32 devices in a mesh: dp: 4 (over y, x), vocab: 8 (over z, core).
Axes of the slice: x: 2, y: 2, z: 4, core: 2. Of those that a mesh axis runs over, the one named last changes fastest.
Arguments:
- hidden: bfloat16 [32, 4608], P('vocab', 'dp'), may hold values from -64 to 64
- embedding: bfloat16 [32768, 4608], P('vocab', 'dp'), may hold values from -4 to 4
- embed_cot: bfloat16 [32, 4608], P('vocab', 'dp'), may hold values from -0.059814453 to 0.059814453
- input_ids: int32 [32], replicated, may hold values from 0 to 32767
- target_ids: int32 [32], replicated, may hold values from 0 to 32767
- seq_of_token: int32 [32], replicated, may hold values from 0 to 7, never falling along the last dimension, each value on 1 to 8 neighbouring positions
- list_of_seq: int32 [8], replicated, may hold values from 0 to 1, as said below
- rank_of_seq: int32 [8], replicated, may hold values from 0 to 3, as said below
Outputs:
- table_grad: bfloat16 [32768, 4608], P('vocab', 'dp')
- hidden_grad: float32 [32, 4608], P('vocab', 'dp')
The draws below stay inside these ranges and needn't reach their ends.
Inputs may be any that keep to these rules, and one draw needn't show every extreme that they name: `list_of_seq`: each of the 2 lists holds exactly 4 sequences. `rank_of_seq`: the sequences of one list carry the ranks 0 to 3, each once; rank 0 is preferred most.
All inputs are finite; a program needn't handle non-finite values.
Results may differ from the reference program's by a relative error of at most 0.0034.
Values may be sent and summed in bfloat16 or wider, within the bound.
No kernel may reach another device: no remote copies, remote signals or barrier semaphores. Data moves between devices by JAX's collectives and lax.ppermute only.
A program may use at most 64 MiB of HBM per device.

```python
import math
import jax
import jax.numpy as jnp
import numpy as np
from jax import lax

D = 4608
VOCAB_DEV = 4096
VOCAB = 32768
TOKENS = 32
LIST_SIZE = 4
SEQS = 8
SEQ_MOST = 8
N_VOCAB = 8


def table_rows(key, row_ids):
    common = jax.random.truncated_normal(jax.random.fold_in(key, 1), -3.5, 3.5, (D,), jnp.float32)
    row_key = jax.random.fold_in(key, 2)

    def one_row(row_id):
        return jax.random.truncated_normal(jax.random.fold_in(row_key, row_id), -3.5, 3.5, (D,), jnp.float32)
    return (jax.vmap(one_row)(row_ids) + common[None, :]) * (6.0 / math.sqrt(2.0 * D))


def draw_embedding(key, part):
    row_ids = jnp.arange(VOCAB, dtype=jnp.int32)
    return table_rows(jax.random.fold_in(key, 1), row_ids).astype(jnp.bfloat16)


def row_scales(key):
    return jnp.exp(jax.random.uniform(jax.random.fold_in(key, 7), (TOKENS, 1), jnp.float32, math.log(0.1), 0.0))


def draw_hidden(key, part):
    base_key = jax.random.fold_in(key, 2)
    scales = row_scales(key)
    return (jax.random.truncated_normal(base_key, -6.0, 6.0, (TOKENS, D), jnp.float32) * scales).astype(jnp.bfloat16)


def ranking(key):
    return jax.random.permutation(jax.random.fold_in(key, 5), SEQS).astype(jnp.int32)


def draw_list_of_seq(key, part):
    return (ranking(key) // LIST_SIZE).astype(jnp.int32)


def draw_rank_of_seq(key, part):
    return (ranking(key) % LIST_SIZE).astype(jnp.int32)


def set_ends(values, stream_key, low, top_value):
    extent = values.shape
    index_at = [jax.random.randint(jax.random.fold_in(stream_key, axis), (), 0, extent[axis]) for axis in range(len(extent))]
    values = values.at[tuple(index_at)].set(low)
    longest = extent.index(max(extent))
    index_at[longest] = (index_at[longest] + 1) % extent[longest]
    return values.at[tuple(index_at)].set(top_value)


def level_of(stream_key, dims, pieces, smallest, largest):
    factor_of, own = 1.0, jax.random.fold_in(stream_key, 6)
    for dim, blocks in pieces:
        steps = jnp.exp(jax.random.uniform(jax.random.fold_in(own, dim), (blocks,), jnp.float32, smallest / len(pieces), largest / len(pieces)))
        factor_of = factor_of * jnp.repeat(steps, dims[dim] // blocks).reshape([-1 if axis == dim else 1 for axis in range(len(dims))])
    return factor_of


def rank_bounds(count, skew):
    weights = [(1 << 20) // math.isqrt(rank ** skew) + 1 for rank in range(1, count + 1)]
    deviation = 1 + sum(weights) // (1 << 30)
    return np.cumsum(np.array([max(1, weight // deviation) for weight in weights]))


def skewed_ids(own_key, shape, count, slope):
    listing = rank_bounds(count, slope)
    ticket = jax.random.randint(jax.random.fold_in(own_key, 1), shape, 0, int(listing[count - 1]))
    standing = jnp.searchsorted(jnp.asarray(listing, jnp.int32), ticket, side="right")
    return jax.random.permutation(jax.random.fold_in(own_key, 2), count)[standing].astype(jnp.int32)


def length_profile(number_of, total, limit, slope):
    portions = [(1 << 20) // math.isqrt(rank ** slope) + 1 for rank in range(2, number_of + 1)]
    spare, holding = total - limit - (number_of - 1), [1] * (number_of - 1)
    while spare > 0:
        free = [i for i in range(number_of - 1) if holding[i] < limit]
        pool, remaining = sum([portions[i] for i in free]), spare
        for i in free:
            addition = min(limit - holding[i], max(1, remaining * portions[i] // pool), spare)
            holding[i] = holding[i] + addition
            spare = spare - addition
    return np.array([limit] + holding)


def ragged_sizes(key, amount, total, limit, slope):
    if amount == 2:
        one = jax.random.randint(key, (), max(1, total - limit), min(limit, total - 1) + 1)
        return jnp.stack([one, total - one])
    sizes = jnp.asarray(length_profile(amount, total, limit, slope), jnp.int32)
    couples = (amount - 1) // 2
    source_of, taker = sizes[1:1 + 2 * couples:2], sizes[2:2 + 2 * couples:2]
    margin = jnp.minimum(source_of - 1, limit - taker)
    moved = jax.random.randint(jax.random.fold_in(key, 1), (couples,), 0, 1 << 20) % (margin + 1)
    sizes = sizes.at[1:1 + 2 * couples:2].set(source_of - moved).at[2:2 + 2 * couples:2].set(taker + moved)
    return sizes[jax.random.permutation(jax.random.fold_in(key, 2), amount)]


def normal_values(own_key, extent, deviation, limit, shards=(), kind=jnp.bfloat16):
    values = jax.random.normal(own_key, extent, jnp.float32) * deviation
    if len(shards) > 0:
        values = level_of(own_key, extent, shards, -0.22, 0.18) * values
    return jnp.clip(values, min=-limit, max=limit).astype(kind)


def setup_inputs(seed: int = 0) -> dict:
    key_list = jax.random.split(jax.random.key(seed), 9)
    hidden = draw_hidden(jax.random.fold_in(key_list[8], 71), 0)
    embedding = draw_embedding(jax.random.fold_in(key_list[8], 71), 0)
    embed_cot = normal_values(key_list[2], (TOKENS, D), 0.01, 0.059814453, ((0, 8), (1, 4)))
    input_ids = set_ends(skewed_ids(key_list[3], (TOKENS,), VOCAB, 2), jax.random.fold_in(key_list[3], 3), 0, VOCAB - 1).astype(jnp.int32)
    target_ids = set_ends(skewed_ids(key_list[4], (TOKENS,), VOCAB, 2), jax.random.fold_in(key_list[4], 3), 0, VOCAB - 1).astype(jnp.int32)
    seq_of_token = jnp.searchsorted(jnp.cumsum(ragged_sizes(key_list[5], SEQS, TOKENS, SEQ_MOST, 2)), jnp.arange(TOKENS), side="right").astype(jnp.int32)
    list_of_seq = draw_list_of_seq(jax.random.fold_in(key_list[8], 71), 0)
    rank_of_seq = draw_rank_of_seq(jax.random.fold_in(key_list[8], 71), 0)
    return {"hidden": hidden, "embedding": embedding, "embed_cot": embed_cot, "input_ids": input_ids, "target_ids": target_ids, "seq_of_token": seq_of_token, "list_of_seq": list_of_seq, "rank_of_seq": rank_of_seq}


preference_scale = 0.5

def list_coef(scores, list_of_seq, rank_of_seq):
    scaled = preference_scale * scores
    same_list = list_of_seq[:, None] == list_of_seq[None, :]
    in_suffix = same_list & (rank_of_seq[None, :] >= rank_of_seq[:, None])
    suffix_max = lax.optimization_barrier(jnp.max(jnp.where(in_suffix, scaled[None, :], scaled[:, None]), axis=1))
    suffix_sum = lax.optimization_barrier(jnp.sum(jnp.where(in_suffix, jnp.exp(jnp.minimum(scaled[None, :] - suffix_max[:, None], 0.0)), 0.0), axis=1))
    suffix_lse = suffix_max + jnp.log(suffix_sum)
    portion = jnp.where(in_suffix, jnp.exp(jnp.minimum(scaled[None, :] - suffix_lse[:, None], 0.0)), 0.0)
    return preference_scale * (lax.optimization_barrier(jnp.sum(portion, axis=0)) - 1.0)

def reference(hidden, embedding, embed_cot, input_ids, target_ids, seq_of_token, list_of_seq, rank_of_seq):
    logits = jnp.dot(hidden, embedding.T, preferred_element_type=jnp.float32)
    row_max = lax.optimization_barrier(jnp.max(logits, axis=1))
    row_sum = lax.optimization_barrier(jnp.sum(jnp.exp(logits - row_max[:, None]), axis=1))
    log_norm = row_max + jnp.log(row_sum)
    vocab_ids = jnp.arange(VOCAB, dtype=jnp.int32)
    target_hit = vocab_ids[None, :] == target_ids[:, None]
    picked = lax.optimization_barrier(jnp.sum(jnp.where(target_hit, logits, 0.0), axis=1))
    logprob = picked - log_norm
    seq_hot = (seq_of_token[None, :] == jnp.arange(SEQS, dtype=jnp.int32)[:, None]).astype(jnp.float32)
    scores = lax.optimization_barrier(jnp.sum(seq_hot * logprob[None, :], axis=1))
    weight = lax.optimization_barrier(jnp.sum(seq_hot * list_coef(scores, list_of_seq, rank_of_seq)[:, None], axis=0))
    grad_logits = (weight[:, None] * (target_hit.astype(jnp.float32) - jnp.exp(logits - log_norm[:, None]))).astype(jnp.bfloat16)
    hidden_grad = jnp.dot(grad_logits, embedding, preferred_element_type=jnp.float32)
    grad_blocks = grad_logits.reshape(TOKENS, N_VOCAB, VOCAB_DEV).transpose(1, 0, 2)
    hidden_wide = hidden.astype(jnp.float32)

    def block_grad(inputs):
        grad_block, block_index = inputs
        head_part = jnp.einsum('tv,td->vd', grad_block.astype(jnp.float32), hidden_wide)
        entries = block_index * VOCAB_DEV + jnp.arange(VOCAB_DEV, dtype=jnp.int32)
        input_hot = (entries[:, None] == input_ids[None, :]).astype(jnp.bfloat16)
        input_part = jnp.dot(input_hot, embed_cot, preferred_element_type=jnp.float32)
        return (head_part + input_part * math.sqrt(D)).astype(jnp.bfloat16)
    table_grad = lax.map(block_grad, (grad_blocks, jnp.arange(N_VOCAB, dtype=jnp.int32))).reshape(VOCAB, D)
    return (table_grad, hidden_grad)
```

```python
import functools
import math

import jax
import jax.numpy as jnp
from jax import lax
from jax.experimental import pallas as pl
from jax.experimental.pallas import tpu as pltpu
from jax.sharding import PartitionSpec as P

f32 = jnp.float32
bf16 = jnp.bfloat16
preference_scale = 0.5
NT = (((1,), (1,)), ((), ()))
TN = (((0,), (0,)), ((), ()))
VM = pl.BlockSpec(memory_space=pltpu.VMEM)
LANES = 128


def swap(value, axis, size, k):
    return lax.ppermute(value, axis, [(i, i ^ k) for i in range(size)])


def halvings(size):
    ks = []
    k = size // 2
    while k:
        ks.append(k)
        k //= 2
    return ks


def doubled(value, axis, size):
    for k in halvings(size):
        value = jnp.concatenate([value, swap(value, axis, size, k)], axis=0)
    return value


def row_of_place(me, places, rows, size):
    block = places // rows
    owner = jnp.full_like(places, me)
    for r, k in enumerate(halvings(size)):
        owner = owner ^ (((block >> r) & 1) * k)
    return owner * rows + places % rows


def as_column(row, picked):
    return jnp.sum(jnp.where(picked, row, jnp.zeros_like(row)), axis=1, keepdims=True)


def place_mask(me, tokens, rows, size):
    here = row_of_place(me, lax.broadcasted_iota(jnp.int32, (tokens, tokens), 0), rows, size)
    return here == lax.broadcasted_iota(jnp.int32, (tokens, tokens), 1)


def ids_column(row, picked):
    return as_column(row.astype(f32), picked).astype(jnp.int32)


def logits_kernel(tile, h_ref, e_ref, a_ref, b_ref):
    half = a_ref.shape[1]
    for start in range(0, 2 * half, tile):
        part = lax.dot_general(
            e_ref[pl.ds(start, tile), :], h_ref[...], NT, preferred_element_type=f32
        )
        ref, at = (a_ref, start) if start < half else (b_ref, start - half)
        ref[:, pl.ds(at, tile)] = part.T


def stats_kernel(size, rows, parts, me_ref, tgt_ref, *refs):
    ins, (l_ref, s_ref) = refs[:-2], refs[-2:]
    tokens, width = l_ref.shape
    half = width // 2
    me = me_ref[0]
    picked = place_mask(me, tokens, rows, size)
    target = ids_column(tgt_ref[...], picked)
    for n in range(2):
        total = ins[n * parts][...]
        for r in ins[n * parts + 1 : (n + 1) * parts]:
            total = total + r[...]
        l_ref[:, pl.ds(n * half, half)] = total
    logits = l_ref[...]
    columns = lax.broadcasted_iota(jnp.int32, logits.shape, 1) + me * width
    top = jnp.max(logits, axis=1, keepdims=True)
    total = jnp.sum(jnp.exp(logits - top), axis=1, keepdims=True)
    pick = jnp.sum(jnp.where(columns == target, logits, 0.0), axis=1, keepdims=True)
    same = lax.broadcasted_iota(jnp.int32, (tokens, s_ref.shape[1]), 0) == lax.broadcasted_iota(
        jnp.int32, (tokens, s_ref.shape[1]), 1
    )
    s_ref[...] = jnp.zeros_like(s_ref)
    for n, column in enumerate((top, total, pick)):
        s_ref[n : n + 1, :] = jnp.sum(jnp.where(same, column, 0.0), axis=0, keepdims=True)


def join_kernel(step, mine_ref, other_ref, out_ref):
    width = mine_ref.shape[1]
    other = other_ref[...]
    lane = lax.broadcasted_iota(jnp.int32, other.shape, 1)
    other = jnp.where(
        (lane // step) % 2 == 1, pltpu.roll(other, step, 1), pltpu.roll(other, width - step, 1)
    )
    mine = mine_ref[...]
    top = jnp.maximum(mine[0:1, :], other[0:1, :])
    out_ref[...] = jnp.zeros_like(out_ref)
    out_ref[0:1, :] = top
    out_ref[1:2, :] = mine[1:2, :] * jnp.exp(mine[0:1, :] - top) + other[1:2, :] * jnp.exp(
        other[0:1, :] - top
    )
    out_ref[2:3, :] = mine[2:3, :] + other[2:3, :]


def list_coef(scaled, lists, ranks):
    count = scaled.shape[1]
    diagonal = lax.broadcasted_iota(jnp.int32, (count, count), 0) == lax.broadcasted_iota(
        jnp.int32, (count, count), 1
    )
    scaled_col = as_column(scaled, diagonal)
    list_col = as_column(lists, diagonal)
    rank_col = as_column(ranks, diagonal)
    in_suffix = (list_col == lists) & (ranks >= rank_col)
    top = jnp.max(jnp.where(in_suffix, scaled, scaled_col), axis=1, keepdims=True)
    total = jnp.sum(
        jnp.where(in_suffix, jnp.exp(jnp.minimum(scaled - top, 0.0)), 0.0), axis=1, keepdims=True
    )
    lse = top + jnp.log(total)
    portion = jnp.where(in_suffix, jnp.exp(jnp.minimum(scaled - lse, 0.0)), 0.0)
    return preference_scale * (jnp.sum(portion, axis=0, keepdims=True) - 1.0)


def grad_kernel(
    size, rows, me_ref, tgt_ref, seq_ref, list_ref, rank_ref, s_ref, l_ref, e_ref, g_ref, keep_ref, send_ref
):
    tokens, width = l_ref.shape
    seqs = list_ref.shape[1]
    me = me_ref[0]
    picked = place_mask(me, tokens, rows, size)
    target = ids_column(tgt_ref[...], picked)
    seq = ids_column(seq_ref[...], picked)
    same = lax.broadcasted_iota(jnp.int32, (tokens, s_ref.shape[1]), 0) == lax.broadcasted_iota(
        jnp.int32, (tokens, s_ref.shape[1]), 1
    )
    top, total, pick = (as_column(s_ref[n : n + 1, :], same) for n in range(3))
    log_norm = top + jnp.log(total)
    seq_hot = seq == lax.broadcasted_iota(jnp.int32, (tokens, seqs), 1)
    scores = jnp.sum(jnp.where(seq_hot, pick - log_norm, 0.0), axis=0, keepdims=True)
    coef = list_coef(
        preference_scale * scores, list_ref[...].astype(f32), rank_ref[...].astype(f32)
    )
    weight = as_column(coef, seq_hot)
    logits = l_ref[...]
    columns = lax.broadcasted_iota(jnp.int32, logits.shape, 1) + me * width
    hit = (columns == target).astype(f32)
    g_ref[...] = (weight * (hit - jnp.exp(logits - log_norm))).astype(bf16)
    part = jnp.dot(g_ref[...], e_ref[...], preferred_element_type=f32)
    keep_ref[...] = part[: tokens // 2]
    send_ref[...] = part[tokens // 2 :]


def bf16_terms(value, count=3):
    import numpy as np

    left, terms = np.float32(value), []
    for _ in range(count):
        term = np.float32(left.astype(jnp.bfloat16))
        terms.append(float(term))
        left = np.float32(left - term)
    return terms


def table_kernel(size, rows, terms, me_ref, ids_ref, g_ref, h_ref, c_ref, out_ref):
    tokens, tile = g_ref.shape
    me = me_ref[0]
    first = me * (tile * pl.num_programs(0)) + pl.program_id(0) * tile
    ids = ids_column(ids_ref[...], place_mask(me, tokens, rows, size))
    columns = lax.broadcasted_iota(jnp.int32, (tokens, tile), 1) + first
    hit = columns == ids
    left = jnp.concatenate(
        [g_ref[...]] + [jnp.where(hit, t, 0.0).astype(bf16) for t in terms], axis=0
    )
    right = jnp.concatenate([h_ref[...]] + [c_ref[...]] * len(terms), axis=0)
    out_ref[...] = lax.dot_general(left, right, TN, preferred_element_type=f32).astype(bf16)


def params(mib):
    return pltpu.CompilerParams(vmem_limit_bytes=mib << 20)


def body(
    hidden, embedding, embed_cot, input_ids, target_ids, seq_of_token, list_of_seq, rank_of_seq,
    *, n_dp, n_vocab, width_all,
):
    rows, depth = hidden.shape
    width = embedding.shape[0]
    half = width // 2
    tokens = rows * n_vocab
    seqs = list_of_seq.shape[0]
    tile = math.gcd(512, half)
    lanes = -(-tokens // LANES) * LANES
    me = lax.axis_index("vocab").astype(jnp.int32).reshape(1)
    smem = pl.BlockSpec(memory_space=pltpu.SMEM)
    tgt, ids, seq = (v.reshape(1, tokens) for v in (target_ids, input_ids, seq_of_token))
    lists, ranks = list_of_seq.reshape(1, seqs), rank_of_seq.reshape(1, seqs)
    table = pltpu.with_memory_space_constraint(embedding, pltpu.VMEM)

    hidden_all = doubled(hidden, "vocab", n_vocab)
    part_a, part_b = pl.pallas_call(
        functools.partial(logits_kernel, tile),
        in_specs=[VM, VM],
        out_specs=(VM, VM),
        out_shape=(jax.ShapeDtypeStruct((tokens, half), f32),) * 2,
        compiler_params=params(12),
        name="logits",
    )(hidden_all, table)

    cot_in, _, _ = lax.optimization_barrier((embed_cot, part_a, part_b))
    cot_all = doubled(cot_in, "vocab", n_vocab)

    order = halvings(n_dp)[::-1]
    pieces = [[part_a], [part_b]]
    for r in range(len(order)):
        ks = (order[r], order[-1 - r])
        others = [swap(sum(p[1:], p[0]), "dp", n_dp, k) for p, k in zip(pieces, ks)]
        pieces = [[sum(p[1:], p[0]), o] for p, o in zip(pieces, others)]
    parts = len(pieces[0])
    logits, stats = pl.pallas_call(
        functools.partial(stats_kernel, n_vocab, rows, parts),
        in_specs=[smem, VM] + [VM] * (2 * parts),
        out_specs=(VM, VM),
        out_shape=(
            jax.ShapeDtypeStruct((tokens, width), f32),
            jax.ShapeDtypeStruct((8, lanes), f32),
        ),
        compiler_params=params(12),
        name="stats",
    )(me, tgt, *pieces[0], *pieces[1])
    for r, k in enumerate(halvings(n_vocab)):
        stats = pl.pallas_call(
            functools.partial(join_kernel, rows << r),
            in_specs=[VM, VM],
            out_specs=VM,
            out_shape=jax.ShapeDtypeStruct(stats.shape, f32),
            compiler_params=params(2),
            name="join",
        )(stats, swap(stats, "vocab", n_vocab, k))

    grad, keep, send = pl.pallas_call(
        functools.partial(grad_kernel, n_vocab, rows),
        in_specs=[smem] + [VM] * 7,
        out_specs=(VM, VM, VM),
        out_shape=(
            jax.ShapeDtypeStruct((tokens, width), bf16),
            jax.ShapeDtypeStruct((tokens // 2, depth), f32),
            jax.ShapeDtypeStruct((tokens // 2, depth), f32),
        ),
        compiler_params=params(12),
        name="grad",
    )(me, tgt, seq, lists, ranks, stats, logits, table)

    back = halvings(n_vocab)[::-1]
    for n, k in enumerate(back):
        other = swap(send, "vocab", n_vocab, k)
        if n + 1 < len(back):
            cut = keep.shape[0] // 2
            send = keep[cut:] + other[cut:]
            keep = keep[:cut] + other[:cut]
        else:
            keep = keep + other
    block = math.gcd(1024, width)
    table_grad = pl.pallas_call(
        functools.partial(table_kernel, n_vocab, rows, bf16_terms(math.sqrt(width_all))),
        grid=(width // block,),
        in_specs=[
            smem,
            pl.BlockSpec((1, tokens), lambda i: (0, 0)),
            pl.BlockSpec((tokens, block), lambda i: (0, i)),
            pl.BlockSpec((tokens, depth), lambda i: (0, 0)),
            pl.BlockSpec((tokens, depth), lambda i: (0, 0)),
        ],
        out_specs=pl.BlockSpec((block, depth), lambda i: (i, 0)),
        out_shape=jax.ShapeDtypeStruct((width, depth), bf16),
        compiler_params=params(24),
        cost_estimate=pl.CostEstimate(
            flops=2 * 128 * width * depth, bytes_accessed=2 * width * depth, transcendentals=0
        ),
        name="table",
    )(me, ids, grad, hidden_all, cot_all)
    return (table_grad, keep)


def solution(mesh):
    n_dp, n_vocab = mesh.shape["dp"], mesh.shape["vocab"]
    placed = (P("vocab", "dp"), P("vocab", "dp"), P("vocab", "dp"), P(), P(), P(), P(), P())

    def whole(hidden, *rest):
        return jax.shard_map(
            functools.partial(body, n_dp=n_dp, n_vocab=n_vocab, width_all=hidden.shape[1]),
            mesh=mesh,
            in_specs=placed,
            out_specs=(P("vocab", "dp"), P("vocab", "dp")),
            check_vma=False,
        )(hidden, *rest)

    return whole
```

```python
import functools
import math

import jax
import jax.numpy as jnp
from jax import lax
from jax.experimental import pallas as pl
from jax.experimental.pallas import tpu as pltpu
from jax.sharding import PartitionSpec as P

f32 = jnp.float32
bf16 = jnp.bfloat16
preference_scale = 0.5
NT = (((1,), (1,)), ((), ()))
TN = (((0,), (0,)), ((), ()))
VM = pl.BlockSpec(memory_space=pltpu.VMEM)
LANES = 128


def swap(value, axis, size, k):
    return lax.ppermute(value, axis, [(i, i ^ k) for i in range(size)])


def halvings(size):
    ks = []
    k = size // 2
    while k:
        ks.append(k)
        k //= 2
    return ks


def joined_kernel(pieces, *refs):
    out_ref = refs[-1]
    at = 0
    for ref in refs[:pieces]:
        rows = ref.shape[0]
        out_ref[at : at + rows, :] = ref[...]
        at += rows


def joined(pieces, extra=()):
    rows = sum(p.shape[0] for p in pieces)
    return pl.pallas_call(
        functools.partial(joined_kernel, len(pieces)),
        in_specs=[VM] * len(pieces) + [pl.BlockSpec(memory_space=pl.ANY)] * len(extra),
        out_specs=VM,
        out_shape=jax.ShapeDtypeStruct((rows,) + pieces[0].shape[1:], pieces[0].dtype),
        compiler_params=params(2),
        name="joined",
    )(*pieces, *extra)


def paired_kernel(h_ref, c_ref, out_ref, h_buf, c_buf, sems):
    depth = h_ref.shape[1]
    gap = out_ref.shape[1] // 2
    bufs = (h_buf, c_buf)
    copies = [
        pltpu.make_async_copy(ref, buf, sems.at[n])
        for n, (ref, buf) in enumerate(zip((h_ref, c_ref), bufs))
    ]
    for copy in copies:
        copy.start()
    if gap != depth:
        out_ref[...] = jnp.zeros_like(out_ref)
    for n, copy in enumerate(copies):
        copy.wait()
        out_ref[:, n * gap : n * gap + depth] = bufs[n][...]


def paired(hidden, cot, gap):
    return pl.pallas_call(
        paired_kernel,
        in_specs=[pl.BlockSpec(memory_space=pltpu.HBM)] * 2,
        out_specs=VM,
        out_shape=jax.ShapeDtypeStruct((hidden.shape[0], 2 * gap), hidden.dtype),
        scratch_shapes=[
            pltpu.VMEM(hidden.shape, hidden.dtype),
            pltpu.VMEM(cot.shape, cot.dtype),
            pltpu.SemaphoreType.DMA((2,)),
        ],
        compiler_params=params(2),
        name="paired",
    )(in_hbm(hidden), in_hbm(cot))


def added_kernel(a_ref, b_ref, out_ref):
    out_ref[...] = a_ref[...] + b_ref[...]


def added(pieces):
    if len(pieces) == 1:
        return pieces[0]
    return pl.pallas_call(
        added_kernel,
        in_specs=[VM, VM],
        out_specs=VM,
        out_shape=jax.ShapeDtypeStruct(pieces[0].shape, pieces[0].dtype),
        compiler_params=params(4),
        name="added",
    )(*pieces)


def in_hbm(value):
    return pltpu.with_memory_space_constraint(value, pltpu.HBM)


def fetch_kernel(start, e_ref, after_ref, out_ref, sem):
    copy = pltpu.make_async_copy(e_ref.at[pl.ds(start, out_ref.shape[0]), :], out_ref, sem)
    copy.start()
    copy.wait()


def fetched(table, start, rows, after):
    return pl.pallas_call(
        functools.partial(fetch_kernel, start),
        in_specs=[pl.BlockSpec(memory_space=pltpu.HBM), pl.BlockSpec(memory_space=pl.ANY)],
        out_specs=VM,
        out_shape=jax.ShapeDtypeStruct((rows, table.shape[1]), table.dtype),
        scratch_shapes=[pltpu.SemaphoreType.DMA],
        compiler_params=params(2),
        cost_estimate=pl.CostEstimate(
            flops=0, bytes_accessed=2 * rows * table.shape[1] * 2, transcendentals=0
        ),
        name="fetched",
    )(table, after)


def row_of_place(me, places, rows, size):
    block = places // rows
    owner = jnp.full_like(places, me)
    for r, k in enumerate(halvings(size)):
        owner = owner ^ (((block >> r) & 1) * k)
    return owner * rows + places % rows


def as_column(row, picked):
    return jnp.sum(jnp.where(picked, row, jnp.zeros_like(row)), axis=1, keepdims=True)


def place_mask(me, tokens, rows, size):
    here = row_of_place(me, lax.broadcasted_iota(jnp.int32, (tokens, tokens), 0), rows, size)
    return here == lax.broadcasted_iota(jnp.int32, (tokens, tokens), 1)


def ids_column(row, picked):
    return as_column(row.astype(f32), picked).astype(jnp.int32)


def logits_kernel(tile, count, h_ref, *refs):
    depth = refs[0].shape[1]
    a_ref = refs[count]
    at = 0
    for e_ref in refs[:count]:
        for start in range(0, e_ref.shape[0], tile):
            part = lax.dot_general(
                e_ref[pl.ds(start, tile), :],
                h_ref[:, :depth],
                NT,
                preferred_element_type=f32,
            )
            a_ref[:, pl.ds(at, tile)] = part.T
            at += tile


def logits_fetch_kernel(tile, count, start, h_ref, *refs):
    table_ref, last_ref, sem = refs[count], refs[count + 2], refs[count + 3]
    copy = pltpu.make_async_copy(
        table_ref.at[pl.ds(start, last_ref.shape[0]), :], last_ref, sem
    )
    copy.start()
    logits_kernel(tile, count, h_ref, *refs[:count], refs[count + 1])
    copy.wait()


def stats_kernel(size, rows, parts, tgt_ref, *refs):
    ins, (l_ref, s_ref) = refs[:-2], refs[-2:]
    tokens, width = l_ref.shape
    half = width // 2
    me = lax.axis_index("vocab")
    picked = place_mask(me, tokens, rows, size)
    target = ids_column(tgt_ref[...], picked)
    for n in range(2):
        total = ins[n * parts][...]
        for r in ins[n * parts + 1 : (n + 1) * parts]:
            total = total + r[...]
        l_ref[:, pl.ds(n * half, half)] = total
    logits = l_ref[...]
    columns = lax.broadcasted_iota(jnp.int32, logits.shape, 1) + me * width
    top = jnp.max(logits, axis=1, keepdims=True)
    total = jnp.sum(jnp.exp(logits - top), axis=1, keepdims=True)
    pick = jnp.sum(jnp.where(columns == target, logits, 0.0), axis=1, keepdims=True)
    same = lax.broadcasted_iota(jnp.int32, (tokens, s_ref.shape[1]), 0) == lax.broadcasted_iota(
        jnp.int32, (tokens, s_ref.shape[1]), 1
    )
    s_ref[...] = jnp.zeros_like(s_ref)
    for n, column in enumerate((top, total, pick)):
        s_ref[n : n + 1, :] = jnp.sum(jnp.where(same, column, 0.0), axis=0, keepdims=True)


def join_kernel(step, mine_ref, other_ref, out_ref):
    width = mine_ref.shape[1]
    other = other_ref[...]
    lane = lax.broadcasted_iota(jnp.int32, other.shape, 1)
    other = jnp.where(
        (lane // step) % 2 == 1, pltpu.roll(other, step, 1), pltpu.roll(other, width - step, 1)
    )
    mine = mine_ref[...]
    top = jnp.maximum(mine[0:1, :], other[0:1, :])
    out_ref[...] = jnp.zeros_like(out_ref)
    out_ref[0:1, :] = top
    out_ref[1:2, :] = mine[1:2, :] * jnp.exp(mine[0:1, :] - top) + other[1:2, :] * jnp.exp(
        other[0:1, :] - top
    )
    out_ref[2:3, :] = mine[2:3, :] + other[2:3, :]


def list_coef(scaled, lists, ranks):
    count = scaled.shape[1]
    diagonal = lax.broadcasted_iota(jnp.int32, (count, count), 0) == lax.broadcasted_iota(
        jnp.int32, (count, count), 1
    )
    scaled_col = as_column(scaled, diagonal)
    list_col = as_column(lists, diagonal)
    rank_col = as_column(ranks, diagonal)
    in_suffix = (list_col == lists) & (ranks >= rank_col)
    top = jnp.max(jnp.where(in_suffix, scaled, scaled_col), axis=1, keepdims=True)
    total = jnp.sum(
        jnp.where(in_suffix, jnp.exp(jnp.minimum(scaled - top, 0.0)), 0.0), axis=1, keepdims=True
    )
    lse = top + jnp.log(total)
    portion = jnp.where(in_suffix, jnp.exp(jnp.minimum(scaled - lse, 0.0)), 0.0)
    return preference_scale * (jnp.sum(portion, axis=0, keepdims=True) - 1.0)


def grad_kernel(
    size, rows, count, tgt_ref, seq_ref, list_ref, rank_ref, s_ref, l_ref, *refs
):
    e_refs, (g_ref, keep_ref, send_ref) = refs[:count], refs[count:]
    tokens, width = l_ref.shape
    seqs = list_ref.shape[1]
    me = lax.axis_index("vocab")
    picked = place_mask(me, tokens, rows, size)
    target = ids_column(tgt_ref[...], picked)
    seq = ids_column(seq_ref[...], picked)
    same = lax.broadcasted_iota(jnp.int32, (tokens, s_ref.shape[1]), 0) == lax.broadcasted_iota(
        jnp.int32, (tokens, s_ref.shape[1]), 1
    )
    top, total, pick = (as_column(s_ref[n : n + 1, :], same) for n in range(3))
    log_norm = top + jnp.log(total)
    seq_hot = seq == lax.broadcasted_iota(jnp.int32, (tokens, seqs), 1)
    scores = jnp.sum(jnp.where(seq_hot, pick - log_norm, 0.0), axis=0, keepdims=True)
    coef = list_coef(
        preference_scale * scores, list_ref[...].astype(f32), rank_ref[...].astype(f32)
    )
    weight = as_column(coef, seq_hot)
    logits = l_ref[...]
    columns = lax.broadcasted_iota(jnp.int32, logits.shape, 1) + me * width
    hit = (columns == target).astype(f32)
    g_ref[...] = (weight * (hit - jnp.exp(logits - log_norm))).astype(bf16)
    part, at = None, 0
    for e_ref in e_refs:
        piece = jnp.dot(
            g_ref[:, pl.ds(at, e_ref.shape[0])], e_ref[...], preferred_element_type=f32
        )
        part = piece if part is None else part + piece
        at += e_ref.shape[0]
    keep_ref[...] = part[: tokens // 2]
    send_ref[...] = part[tokens // 2 :]


def bf16_terms(value, count=3):
    import numpy as np

    left, terms = np.float32(value), []
    for _ in range(count):
        term = np.float32(left.astype(jnp.bfloat16))
        terms.append(float(term))
        left = np.float32(left - term)
    return terms


def table_kernel(size, rows, terms, tile, ids_ref, g_ref, hc_ref, out_ref, buf, sems):
    tokens, width = g_ref.shape
    depth = out_ref.shape[1]
    gap = hc_ref.shape[1] // 2
    me = lax.axis_index("vocab")
    ids = ids_column(ids_ref[...], place_mask(me, tokens, rows, size)) - me * width
    right = jnp.concatenate(
        [hc_ref[:, :depth]] + [hc_ref[:, gap : gap + depth]] * len(terms), axis=0
    )
    copies = []
    for n in range(width // tile):
        hit = lax.broadcasted_iota(jnp.int32, (tokens, tile), 1) + n * tile == ids
        left = jnp.concatenate(
            [g_ref[:, pl.ds(n * tile, tile)]]
            + [jnp.where(hit, t, 0.0).astype(bf16) for t in terms],
            axis=0,
        )
        buf[pl.ds(n * tile, tile), :] = lax.dot_general(
            left, right, TN, preferred_element_type=f32
        ).astype(bf16)
        at = pl.ds(n * tile, tile)
        copies.append(pltpu.make_async_copy(buf.at[at], out_ref.at[at], sems.at[n]))
        copies[-1].start()
    for copy in copies:
        copy.wait()


def params(mib):
    return pltpu.CompilerParams(vmem_limit_bytes=mib << 20)


def body(
    hidden, embedding, embed_cot, input_ids, target_ids, seq_of_token, list_of_seq, rank_of_seq,
    *, n_dp, n_vocab, width_all,
):
    rows, depth = hidden.shape
    width = embedding.shape[0]
    half = width // 2
    tokens = rows * n_vocab
    seqs = list_of_seq.shape[0]
    tile = math.gcd(512, half)
    lanes = -(-tokens // LANES) * LANES
    tgt, ids, seq = (v.reshape(1, tokens) for v in (target_ids, input_ids, seq_of_token))
    lists, ranks = list_of_seq.reshape(1, seqs), rank_of_seq.reshape(1, seqs)
    gap = -(-depth // LANES) * LANES
    quarter = width // 4
    embedding = in_hbm(embedding)

    gathered = [paired(hidden, embed_cot, gap)]
    after, fetches = gathered[0], []
    for n, k in enumerate(halvings(n_vocab)):
        other = swap(after, "vocab", n_vocab, k)
        if len(fetches) < 3:
            fetches.append(fetched(embedding, len(fetches) * quarter, quarter, after))
            after = joined(gathered + [other], fetches[-1:])
        else:
            after = joined(gathered + [other])
        gathered = [after]
    both = after
    while len(fetches) < 3:
        fetches.append(fetched(embedding, len(fetches) * quarter, quarter, after))
    part_a, last = pl.pallas_call(
        functools.partial(logits_fetch_kernel, tile, 2, 3 * quarter),
        in_specs=[VM] * 3 + [pl.BlockSpec(memory_space=pltpu.HBM)],
        out_specs=(VM, VM),
        out_shape=(
            jax.ShapeDtypeStruct((tokens, half), f32),
            jax.ShapeDtypeStruct((quarter, depth), bf16),
        ),
        scratch_shapes=[pltpu.SemaphoreType.DMA],
        compiler_params=params(12),
        name="logits_a",
    )(both, *fetches[:2], embedding)
    table = [*fetches, last]
    part_b = pl.pallas_call(
        functools.partial(logits_kernel, tile, 2),
        in_specs=[VM] * 3,
        out_specs=VM,
        out_shape=jax.ShapeDtypeStruct((tokens, half), f32),
        compiler_params=params(12),
        name="logits_b",
    )(both, *table[2:])

    order = halvings(n_dp)[::-1]
    pieces = [[part_a], [part_b]]
    for r in range(len(order)):
        ks = (order[r], order[-1 - r])
        pairs = [
            (d * n_vocab + v, (d ^ ks[v % 2]) * n_vocab + v)
            for d in range(n_dp)
            for v in range(n_vocab)
        ]
        for n in range(2):
            total = added(pieces[n])
            pieces[n] = [total, lax.ppermute(total, ("dp", "vocab"), pairs)]
    parts = len(pieces[0])
    logits, stats = pl.pallas_call(
        functools.partial(stats_kernel, n_vocab, rows, parts),
        in_specs=[VM] * (1 + 2 * parts),
        out_specs=(VM, VM),
        out_shape=(
            jax.ShapeDtypeStruct((tokens, width), f32),
            jax.ShapeDtypeStruct((8, lanes), f32),
        ),
        compiler_params=params(12),
        name="stats",
    )(tgt, *pieces[0], *pieces[1])
    for r, k in enumerate(halvings(n_vocab)):
        stats = pl.pallas_call(
            functools.partial(join_kernel, rows << r),
            in_specs=[VM, VM],
            out_specs=VM,
            out_shape=jax.ShapeDtypeStruct(stats.shape, f32),
            compiler_params=params(2),
            name="join",
        )(stats, swap(stats, "vocab", n_vocab, k))

    grad, keep, send = pl.pallas_call(
        functools.partial(grad_kernel, n_vocab, rows, len(table)),
        in_specs=[VM] * (6 + len(table)),
        out_specs=(VM, VM, VM),
        out_shape=(
            jax.ShapeDtypeStruct((tokens, width), bf16),
            jax.ShapeDtypeStruct((tokens // 2, depth), f32),
            jax.ShapeDtypeStruct((tokens // 2, depth), f32),
        ),
        compiler_params=params(12),
        name="grad",
    )(tgt, seq, lists, ranks, stats, logits, *table)

    back = halvings(n_vocab)[::-1]
    for n, k in enumerate(back):
        other = swap(send, "vocab", n_vocab, k)
        if n + 1 < len(back):
            cut = keep.shape[0] // 2
            send = keep[cut:] + other[cut:]
            keep = keep[:cut] + other[:cut]
        else:
            keep = keep + other
    block = math.gcd(512, width)
    table_grad = pl.pallas_call(
        functools.partial(table_kernel, n_vocab, rows, bf16_terms(math.sqrt(width_all)), block),
        in_specs=[VM, VM, VM],
        out_specs=pl.BlockSpec(memory_space=pltpu.HBM),
        out_shape=jax.ShapeDtypeStruct((width, depth), bf16),
        scratch_shapes=[
            pltpu.VMEM((width, depth), bf16),
            pltpu.SemaphoreType.DMA((width // block,)),
        ],
        compiler_params=params(24),
        cost_estimate=pl.CostEstimate(
            flops=2 * 128 * width * depth, bytes_accessed=2 * width * depth, transcendentals=0
        ),
        name="table",
    )(ids, grad, both)
    return (table_grad, keep)


def solution(mesh):
    n_dp, n_vocab = mesh.shape["dp"], mesh.shape["vocab"]
    placed = (P("vocab", "dp"), P("vocab", "dp"), P("vocab", "dp"), P(), P(), P(), P(), P())

    def whole(hidden, *rest):
        return jax.shard_map(
            functools.partial(body, n_dp=n_dp, n_vocab=n_vocab, width_all=hidden.shape[1]),
            mesh=mesh,
            in_specs=placed,
            out_specs=(P("vocab", "dp"), P("vocab", "dp")),
            check_vma=False,
        )(hidden, *rest)

    return whole
```

```python
import functools
import math

import jax
import jax.numpy as jnp
from jax import lax
from jax.experimental import pallas as pl
from jax.experimental.pallas import tpu as pltpu
from jax.sharding import PartitionSpec as P

f32 = jnp.float32
bf16 = jnp.bfloat16
preference_scale = 0.5
NT = (((1,), (1,)), ((), ()))
TN = (((0,), (0,)), ((), ()))
VM = pl.BlockSpec(memory_space=pltpu.VMEM)
LANES = 128


def swap(value, axis, size, k):
    return lax.ppermute(value, axis, [(i, i ^ k) for i in range(size)])


def halvings(size):
    ks = []
    k = size // 2
    while k:
        ks.append(k)
        k //= 2
    return ks


def joined_kernel(pieces, *refs):
    out_ref = refs[-1]
    at = 0
    for ref in refs[:pieces]:
        rows = ref.shape[0]
        out_ref[at : at + rows, :] = ref[...]
        at += rows


def joined(pieces, extra=()):
    rows = sum(p.shape[0] for p in pieces)
    return pl.pallas_call(
        functools.partial(joined_kernel, len(pieces)),
        in_specs=[VM] * len(pieces) + [pl.BlockSpec(memory_space=pl.ANY)] * len(extra),
        out_specs=VM,
        out_shape=jax.ShapeDtypeStruct((rows,) + pieces[0].shape[1:], pieces[0].dtype),
        compiler_params=params(2),
        name="joined",
    )(*pieces, *extra)


def paired_kernel(h_ref, c_ref, out_ref, h_buf, c_buf, sems):
    depth = h_ref.shape[1]
    gap = out_ref.shape[1] // 2
    bufs = (h_buf, c_buf)
    copies = [
        pltpu.make_async_copy(ref, buf, sems.at[n])
        for n, (ref, buf) in enumerate(zip((h_ref, c_ref), bufs))
    ]
    for copy in copies:
        copy.start()
    if gap != depth:
        out_ref[...] = jnp.zeros_like(out_ref)
    for n, copy in enumerate(copies):
        copy.wait()
        out_ref[:, n * gap : n * gap + depth] = bufs[n][...]


def paired(hidden, cot, gap):
    return pl.pallas_call(
        paired_kernel,
        in_specs=[pl.BlockSpec(memory_space=pltpu.HBM)] * 2,
        out_specs=VM,
        out_shape=jax.ShapeDtypeStruct((hidden.shape[0], 2 * gap), hidden.dtype),
        scratch_shapes=[
            pltpu.VMEM(hidden.shape, hidden.dtype),
            pltpu.VMEM(cot.shape, cot.dtype),
            pltpu.SemaphoreType.DMA((2,)),
        ],
        compiler_params=params(2),
        name="paired",
    )(in_hbm(hidden), in_hbm(cot))


def added_kernel(a_ref, b_ref, out_ref):
    out_ref[...] = a_ref[...] + b_ref[...]


def added(pieces):
    if len(pieces) == 1:
        return pieces[0]
    return pl.pallas_call(
        added_kernel,
        in_specs=[VM, VM],
        out_specs=VM,
        out_shape=jax.ShapeDtypeStruct(pieces[0].shape, pieces[0].dtype),
        compiler_params=params(4),
        name="added",
    )(*pieces)


def in_hbm(value):
    return pltpu.with_memory_space_constraint(value, pltpu.HBM)


def fetch_kernel(start, e_ref, after_ref, out_ref, sem):
    copy = pltpu.make_async_copy(e_ref.at[pl.ds(start, out_ref.shape[0]), :], out_ref, sem)
    copy.start()
    copy.wait()


def fetched(table, start, rows, after):
    return pl.pallas_call(
        functools.partial(fetch_kernel, start),
        in_specs=[pl.BlockSpec(memory_space=pltpu.HBM), pl.BlockSpec(memory_space=pl.ANY)],
        out_specs=VM,
        out_shape=jax.ShapeDtypeStruct((rows, table.shape[1]), table.dtype),
        scratch_shapes=[pltpu.SemaphoreType.DMA],
        compiler_params=params(2),
        cost_estimate=pl.CostEstimate(
            flops=0, bytes_accessed=2 * rows * table.shape[1] * 2, transcendentals=0
        ),
        name="fetched",
    )(table, after)


def row_of_place(me, places, rows, size):
    block = places // rows
    owner = jnp.full_like(places, me)
    for r, k in enumerate(halvings(size)):
        owner = owner ^ (((block >> r) & 1) * k)
    return owner * rows + places % rows


def as_column(row, picked):
    return jnp.sum(jnp.where(picked, row, jnp.zeros_like(row)), axis=1, keepdims=True)


def place_mask(me, tokens, rows, size):
    here = row_of_place(me, lax.broadcasted_iota(jnp.int32, (tokens, tokens), 0), rows, size)
    return here == lax.broadcasted_iota(jnp.int32, (tokens, tokens), 1)


def ids_column(row, picked):
    return as_column(row.astype(f32), picked).astype(jnp.int32)


def logits_kernel(tile, count, h_ref, *refs):
    depth = refs[0].shape[1]
    a_ref = refs[count]
    at = 0
    for e_ref in refs[:count]:
        for start in range(0, e_ref.shape[0], tile):
            part = lax.dot_general(
                e_ref[pl.ds(start, tile), :],
                h_ref[:, :depth],
                NT,
                preferred_element_type=f32,
            )
            a_ref[:, pl.ds(at, tile)] = part.T
            at += tile


def logits_fetch_kernel(tile, count, start, h_ref, *refs):
    table_ref, last_ref, sem = refs[count], refs[count + 2], refs[count + 3]
    copy = pltpu.make_async_copy(
        table_ref.at[pl.ds(start, last_ref.shape[0]), :], last_ref, sem
    )
    copy.start()
    logits_kernel(tile, count, h_ref, *refs[:count], refs[count + 1])
    copy.wait()


def diagonal(rows, columns):
    return lax.broadcasted_iota(jnp.int32, (rows, columns), 0) == lax.broadcasted_iota(
        jnp.int32, (rows, columns), 1
    )


def soft_kernel(size, rows, parts, count, tgt_ref, *refs):
    ins, e_refs = refs[: 2 * parts], refs[2 * parts : 2 * parts + count]
    l_ref, keep_ref, send_ref, left_ref = refs[2 * parts + count :]
    tokens, width = l_ref.shape
    depth = e_refs[0].shape[1]
    half = width // 2
    me = lax.axis_index("vocab")
    target = ids_column(tgt_ref[...], place_mask(me, tokens, rows, size)) - me * width
    for n in range(2):
        total = ins[n * parts][...]
        for r in ins[n * parts + 1 : (n + 1) * parts]:
            total = total + r[...]
        l_ref[:, pl.ds(n * half, half)] = total
    logits = l_ref[...]
    hit = lax.broadcasted_iota(jnp.int32, logits.shape, 1) == target
    top = jnp.max(logits, axis=1, keepdims=True)
    share = jnp.exp(logits - top)
    total = jnp.sum(share, axis=1, keepdims=True)
    pick = jnp.sum(jnp.where(hit, logits, 0.0), axis=1, keepdims=True)
    left_ref[:tokens, :] = jnp.where(hit, 0.0, share).astype(bf16)
    left_ref[tokens:, :] = hit.astype(f32).astype(bf16)
    part, at = None, 0
    for e_ref in e_refs:
        piece = jnp.dot(
            left_ref[:, pl.ds(at, e_ref.shape[0])], e_ref[...], preferred_element_type=f32
        )
        part = piece if part is None else part + piece
        at += e_ref.shape[0]
    lanes = -(-tokens // LANES) * LANES
    gap = (keep_ref.shape[1] - lanes) // 2
    same = diagonal(tokens, lanes)
    stats = [
        jnp.sum(jnp.where(same, column, 0.0), axis=0, keepdims=True)
        for column in (top, total, pick)
    ]
    n = tokens // 2
    for at, ref in ((n, send_ref), (0, keep_ref)):
        if gap != depth:
            ref[...] = jnp.zeros_like(ref)
        ref[:, :depth] = part[at : at + n]
        ref[:, gap : gap + depth] = part[tokens + at : tokens + at + n]
        ref[:, 2 * gap :] = jnp.zeros((n, lanes), f32)
        for i, row in enumerate(stats):
            ref[i : i + 1, 2 * gap :] = row


def merged(step, lanes, mine_ref, other_ref):
    count = mine_ref.shape[0]
    gap = (mine_ref.shape[1] - lanes) // 2
    lane = lax.broadcasted_iota(jnp.int32, (1, lanes), 1)

    def aligned(row):
        row = jnp.broadcast_to(row, (8, lanes))
        turned = jnp.where(
            (lax.broadcasted_iota(jnp.int32, row.shape, 1) // step) % 2 == 1,
            pltpu.roll(row, step, 1),
            pltpu.roll(row, lanes - step, 1),
        )
        return turned[0:1, :]

    mine = [mine_ref[i : i + 1, 2 * gap :] for i in range(3)]
    other = [aligned(other_ref[i : i + 1, 2 * gap :]) for i in range(3)]
    top = jnp.maximum(mine[0], other[0])
    scale_mine, scale_other = jnp.exp(mine[0] - top), jnp.exp(other[0] - top)
    total = mine[1] * scale_mine + other[1] * scale_other
    same = diagonal(count, lanes)
    products = mine_ref[:, :gap] * as_column(scale_mine, same) + other_ref[
        :, :gap
    ] * as_column(scale_other, same)
    rows = mine_ref[:, gap : 2 * gap] + other_ref[:, gap : 2 * gap]
    return products, rows, (top, total, mine[2] + other[2])


def join_kernel(step, lanes, mine_ref, other_ref, keep_ref, send_ref):
    products, rows, stats = merged(step, lanes, mine_ref, other_ref)
    n = keep_ref.shape[0]
    gap = products.shape[1]
    for at, ref in ((n, send_ref), (0, keep_ref)):
        ref[:, :gap] = products[at : at + n]
        ref[:, gap : 2 * gap] = rows[at : at + n]
        ref[:, 2 * gap :] = jnp.zeros((n, lanes), f32)
        for i, row in enumerate(stats):
            ref[i : i + 1, 2 * gap :] = row


def list_coef(scaled, lists, ranks):
    count = scaled.shape[1]
    diagonal = lax.broadcasted_iota(jnp.int32, (count, count), 0) == lax.broadcasted_iota(
        jnp.int32, (count, count), 1
    )
    scaled_col = as_column(scaled, diagonal)
    list_col = as_column(lists, diagonal)
    rank_col = as_column(ranks, diagonal)
    in_suffix = (list_col == lists) & (ranks >= rank_col)
    top = jnp.max(jnp.where(in_suffix, scaled, scaled_col), axis=1, keepdims=True)
    total = jnp.sum(
        jnp.where(in_suffix, jnp.exp(jnp.minimum(scaled - top, 0.0)), 0.0), axis=1, keepdims=True
    )
    lse = top + jnp.log(total)
    portion = jnp.where(in_suffix, jnp.exp(jnp.minimum(scaled - lse, 0.0)), 0.0)
    return preference_scale * (jnp.sum(portion, axis=0, keepdims=True) - 1.0)


def bf16_terms(value, count=3):
    import numpy as np

    left, terms = np.float32(value), []
    for _ in range(count):
        term = np.float32(left.astype(jnp.bfloat16))
        terms.append(float(term))
        left = np.float32(left - term)
    return terms


def table_kernel(
    size, rows, terms, tile, step,
    tgt_ref, ids_ref, seq_ref, list_ref, rank_ref, mine_ref, other_ref, l_ref, hc_ref,
    out_ref, hid_ref, buf, hid_buf, sems, hid_sem,
):
    tokens, width = l_ref.shape
    depth = out_ref.shape[1]
    gap = hc_ref.shape[1] // 2
    lanes = mine_ref.shape[1] - 2 * gap
    seqs = list_ref.shape[1]
    me = lax.axis_index("vocab")
    picked = place_mask(me, tokens, rows, size)
    target = ids_column(tgt_ref[...], picked) - me * width
    ids = ids_column(ids_ref[...], picked) - me * width
    seq = ids_column(seq_ref[...], picked)
    products, hit_rows, stats = merged(step, lanes, mine_ref, other_ref)
    same = diagonal(tokens, lanes)
    top, total, pick = (as_column(row, same) for row in stats)
    log_norm = top + jnp.log(total)
    seq_hot = seq == lax.broadcasted_iota(jnp.int32, (tokens, seqs), 1)
    scores = jnp.sum(jnp.where(seq_hot, pick - log_norm, 0.0), axis=0, keepdims=True)
    coef = list_coef(
        preference_scale * scores, list_ref[...].astype(f32), rank_ref[...].astype(f32)
    )
    weight = as_column(coef, seq_hot)
    at_target = (weight * (1.0 - jnp.exp(pick - log_norm))).astype(bf16).astype(f32)
    elsewhere = weight * jnp.exp(top - log_norm)
    hid_buf[...] = (at_target[:rows] * hit_rows - elsewhere[:rows] * products)[:, :depth]
    hid_copy = pltpu.make_async_copy(hid_buf, hid_ref, hid_sem)
    hid_copy.start()
    right = jnp.concatenate(
        [hc_ref[:, :depth]] + [hc_ref[:, gap : gap + depth]] * len(terms), axis=0
    )
    copies = []
    for n in range(width // tile):
        columns = lax.broadcasted_iota(jnp.int32, (tokens, tile), 1) + n * tile
        share = jnp.exp(l_ref[:, pl.ds(n * tile, tile)] - log_norm)
        grad = (weight * ((columns == target).astype(f32) - share)).astype(bf16)
        hot = columns == ids
        left = jnp.concatenate(
            [grad] + [jnp.where(hot, t, 0.0).astype(bf16) for t in terms], axis=0
        )
        at = pl.ds(n * tile, tile)
        buf[at, :] = lax.dot_general(left, right, TN, preferred_element_type=f32).astype(bf16)
        copies.append(pltpu.make_async_copy(buf.at[at], out_ref.at[at], sems.at[n]))
        copies[-1].start()
    hid_copy.wait()
    for copy in copies:
        copy.wait()


def params(mib):
    return pltpu.CompilerParams(vmem_limit_bytes=mib << 20)


def body(
    hidden, embedding, embed_cot, input_ids, target_ids, seq_of_token, list_of_seq, rank_of_seq,
    *, n_dp, n_vocab, width_all,
):
    rows, depth = hidden.shape
    width = embedding.shape[0]
    half = width // 2
    tokens = rows * n_vocab
    seqs = list_of_seq.shape[0]
    tile = math.gcd(512, half)
    lanes = -(-tokens // LANES) * LANES
    tgt, ids, seq = (v.reshape(1, tokens) for v in (target_ids, input_ids, seq_of_token))
    lists, ranks = list_of_seq.reshape(1, seqs), rank_of_seq.reshape(1, seqs)
    gap = -(-depth // LANES) * LANES
    quarter = width // 4
    embedding = in_hbm(embedding)

    gathered = [paired(hidden, embed_cot, gap)]
    after, fetches = gathered[0], []
    for n, k in enumerate(halvings(n_vocab)):
        other = swap(after, "vocab", n_vocab, k)
        if len(fetches) < 3:
            fetches.append(fetched(embedding, len(fetches) * quarter, quarter, after))
            after = joined(gathered + [other], fetches[-1:])
        else:
            after = joined(gathered + [other])
        gathered = [after]
    both = after
    while len(fetches) < 3:
        fetches.append(fetched(embedding, len(fetches) * quarter, quarter, after))
    with jax.named_scope("logits_a"):
        part_a, last = pl.pallas_call(
            functools.partial(logits_fetch_kernel, tile, 2, 3 * quarter),
            in_specs=[VM] * 3 + [pl.BlockSpec(memory_space=pltpu.HBM)],
            out_specs=(VM, VM),
            out_shape=(
                jax.ShapeDtypeStruct((tokens, half), f32),
                jax.ShapeDtypeStruct((quarter, depth), bf16),
            ),
            scratch_shapes=[pltpu.SemaphoreType.DMA],
            compiler_params=params(12),
            name="logits_a",
        )(both, *fetches[:2], embedding)
    table = [*fetches, last]
    with jax.named_scope("logits_b"):
        part_b = pl.pallas_call(
            functools.partial(logits_kernel, tile, 2),
            in_specs=[VM] * 3,
            out_specs=VM,
            out_shape=jax.ShapeDtypeStruct((tokens, half), f32),
            compiler_params=params(12),
            name="logits_b",
        )(both, *table[2:])

    order = halvings(n_dp)[::-1]
    pieces = [[part_a], [part_b]]
    for r in range(len(order)):
        ks = (order[r], order[-1 - r])
        pairs = [
            (d * n_vocab + v, (d ^ ks[v % 2]) * n_vocab + v)
            for d in range(n_dp)
            for v in range(n_vocab)
        ]
        for n in range(2):
            total = added(pieces[n])
            with jax.named_scope(f"dp_{n}_{r}"):
                pieces[n] = [total, lax.ppermute(total, ("dp", "vocab"), pairs)]
    parts = len(pieces[0])
    packed = 2 * gap + lanes
    logits, keep, send = pl.pallas_call(
        functools.partial(soft_kernel, n_vocab, rows, parts, len(table)),
        in_specs=[VM] * (1 + 2 * parts + len(table)),
        out_specs=(VM, VM, VM),
        out_shape=(
            jax.ShapeDtypeStruct((tokens, width), f32),
            jax.ShapeDtypeStruct((tokens // 2, packed), f32),
            jax.ShapeDtypeStruct((tokens // 2, packed), f32),
        ),
        scratch_shapes=[pltpu.VMEM((2 * tokens, width), bf16)],
        compiler_params=params(14),
        name="soft",
    )(tgt, *pieces[0], *pieces[1], *table)

    back = halvings(n_vocab)[::-1]
    for n, k in enumerate(back):
        other = swap(send, "vocab", n_vocab, k)
        step = rows * (n_vocab >> (n + 1))
        if n + 1 < len(back):
            shape = jax.ShapeDtypeStruct((keep.shape[0] // 2, packed), f32)
            keep, send = pl.pallas_call(
                functools.partial(join_kernel, step, lanes),
                in_specs=[VM, VM],
                out_specs=(VM, VM),
                out_shape=(shape, shape),
                compiler_params=params(4),
                name="join",
            )(keep, other)
    block = math.gcd(512, width)
    hbm = pl.BlockSpec(memory_space=pltpu.HBM)
    return pl.pallas_call(
        functools.partial(
            table_kernel, n_vocab, rows, bf16_terms(math.sqrt(width_all)), block, step
        ),
        in_specs=[VM] * 9,
        out_specs=(hbm, hbm),
        out_shape=(
            jax.ShapeDtypeStruct((width, depth), bf16),
            jax.ShapeDtypeStruct((rows, depth), f32),
        ),
        scratch_shapes=[
            pltpu.VMEM((width, depth), bf16),
            pltpu.VMEM((rows, depth), f32),
            pltpu.SemaphoreType.DMA((width // block,)),
            pltpu.SemaphoreType.DMA,
        ],
        compiler_params=params(24),
        name="table",
    )(tgt, ids, seq, lists, ranks, keep, other, logits, both)


def solution(mesh):
    n_dp, n_vocab = mesh.shape["dp"], mesh.shape["vocab"]
    placed = (P("vocab", "dp"), P("vocab", "dp"), P("vocab", "dp"), P(), P(), P(), P(), P())

    def whole(hidden, *rest):
        return jax.shard_map(
            functools.partial(body, n_dp=n_dp, n_vocab=n_vocab, width_all=hidden.shape[1]),
            mesh=mesh,
            in_specs=placed,
            out_specs=(P("vocab", "dp"), P("vocab", "dp")),
            check_vma=False,
        )(hidden, *rest)

    return whole
```
